32 devices in a mesh: gx: 4 (over x, core), gy: 8 (over z, y).
Axes of the slice: x: 2, y: 2, z: 4, core: 2. Of those that a mesh axis runs over, the one named last changes fastest.
Arguments:
- fields: float32 [9, 32, 128, 128], P(None, 'gx', 'gy'), may hold values from -6 to 6
- labels: int32 [32, 128, 128], P('gx', 'gy'), may hold values from 0 to 7
- buoyancy: float32 [8], replicated, may hold values from 0.15 to 0.35
- lame_first: float32 [8], replicated, may hold values from 0.15 to 0.45
- shear_modulus: float32 [8], replicated, may hold values from 0.05 to 0.2
- relax_rate: float32 [8], replicated, may hold values from 0.02 to 0.3
Outputs:
- advanced: float32 [9, 32, 128, 128], P(None, 'gx', 'gy')
The draws below stay inside these ranges and needn't reach their ends.
Inputs may be any that keep to these rules, and one draw needn't show every extreme that they name: labels name tissue classes.
All inputs are finite; a program needn't handle non-finite values.
Results may differ from the reference program's by a relative error of at most 0.00002.
Values sent between devices are 32-bit elements; how exact they have to be, the bound alone decides.
A program may use at most 64 MiB of HBM per device.

```python
import math
import jax
import jax.numpy as jnp
from jax import lax

NZ = 128
STEPS = 4
LABELS = 8
NX = 32
NY = 128


def touch_ends(drawn, own_key, least, largest):
    shape = drawn.shape
    index_at = [jax.random.randint(jax.random.fold_in(own_key, axis), (), 0, shape[axis]) for axis in range(len(shape))]
    drawn = drawn.at[tuple(index_at)].set(least)
    longest = shape.index(max(shape))
    index_at[longest] = (index_at[longest] + 1) % shape[longest]
    return drawn.at[tuple(index_at)].set(largest)


def shard_levels(stream_key, extent, pieces, low, high):
    loudness, own = 1.0, jax.random.fold_in(stream_key, 6)
    for position, blocks in pieces:
        draws = jnp.exp(jax.random.uniform(jax.random.fold_in(own, position), (blocks,), jnp.float32, low / len(pieces), high / len(pieces)))
        loudness = loudness * jnp.repeat(draws, extent[position] // blocks).reshape([-1 if axis == position else 1 for axis in range(len(extent))])
    return loudness


def centred(own_key, extent, deviation, most, shards=(), kind=jnp.bfloat16):
    values = deviation * jax.random.normal(own_key, extent, jnp.float32)
    if shards:
        values = values * shard_levels(own_key, extent, shards, -0.22, 0.18)
    return jnp.clip(values, -most, most).astype(kind)


def setup_inputs(seed: int = 0) -> dict:
    seeds = jax.random.split(jax.random.key(seed), 7)
    fields = centred(seeds[0], (9, NX, NY, NZ), 1.0, 6.0, ((1, 4), (2, 8)), jnp.float32)
    labels = touch_ends(jax.random.randint(seeds[1], (NX, NY, NZ), 0, LABELS), jax.random.fold_in(seeds[1], 1), 0, LABELS - 1).astype(jnp.int32)
    buoyancy = jnp.clip(jnp.exp(jax.random.uniform(seeds[2], (LABELS,), jnp.float32, math.log(0.15), math.log(0.35))), 0.15, 0.35)
    lame_first = jnp.clip(jnp.exp(jax.random.uniform(seeds[3], (LABELS,), jnp.float32, math.log(0.15), math.log(0.45))), 0.15, 0.45)
    shear_modulus = jnp.clip(jnp.exp(jax.random.uniform(seeds[4], (LABELS,), jnp.float32, math.log(0.05), math.log(0.2))), 0.05, 0.2)
    relax_rate = jnp.clip(jnp.exp(jax.random.uniform(seeds[5], (LABELS,), jnp.float32, math.log(0.02), math.log(0.3))), 0.02, 0.3)
    return dict(fields=fields, labels=labels, buoyancy=buoyancy, lame_first=lame_first, shear_modulus=shear_modulus, relax_rate=relax_rate)


def ahead(field, axis):
    count = field.shape[axis]
    zeros = jnp.zeros_like(lax.slice_in_dim(field, 0, 1, axis=axis))
    following = jnp.concatenate([lax.slice_in_dim(field, 1, count, axis=axis), zeros], axis)
    return following - field


def behind(field, axis):
    count = field.shape[axis]
    zeros = jnp.zeros_like(lax.slice_in_dim(field, 0, 1, axis=axis))
    previous = jnp.concatenate([zeros, lax.slice_in_dim(field, 0, count - 1, axis=axis)], axis)
    return field - previous


def advance(state, moduli, inside):
    speed_x, speed_y, speed_z, stress_xx, stress_yy, stress_zz, stress_xy, stress_xz, stress_yz = state
    buoy, lame, shear, relax = moduli
    speed_x = (speed_x + buoy * (ahead(stress_xx, 0) + behind(stress_xy, 1) + behind(stress_xz, 2))) * inside
    speed_y = (speed_y + buoy * (behind(stress_xy, 0) + ahead(stress_yy, 1) + behind(stress_yz, 2))) * inside
    speed_z = (speed_z + buoy * (behind(stress_xz, 0) + behind(stress_yz, 1) + ahead(stress_zz, 2))) * inside
    strain_xx = behind(speed_x, 0)
    strain_yy = behind(speed_y, 1)
    strain_zz = behind(speed_z, 2)
    spread = strain_xx + strain_yy + strain_zz
    keep = 1.0 - relax
    stress_xx = (keep * stress_xx + lame * spread + 2.0 * shear * strain_xx) * inside
    stress_yy = (keep * stress_yy + lame * spread + 2.0 * shear * strain_yy) * inside
    stress_zz = (keep * stress_zz + lame * spread + 2.0 * shear * strain_zz) * inside
    stress_xy = (keep * stress_xy + shear * (ahead(speed_x, 1) + ahead(speed_y, 0))) * inside
    stress_xz = (keep * stress_xz + shear * (ahead(speed_x, 2) + ahead(speed_z, 0))) * inside
    stress_yz = (keep * stress_yz + shear * (ahead(speed_y, 2) + ahead(speed_z, 1))) * inside
    return [speed_x, speed_y, speed_z, stress_xx, stress_yy, stress_zz, stress_xy, stress_xz, stress_yz]


def reference(fields, labels, buoyancy, lame_first, shear_modulus, relax_rate):
    moduli = [buoyancy[labels], lame_first[labels], shear_modulus[labels], relax_rate[labels]]
    state = [fields[channel] for channel in range(9)]
    for repeat in range(STEPS):
        state = advance(state, moduli, jnp.float32(1.0))
    return jnp.stack(state)
```

```python
import functools

import jax
import jax.numpy as jnp
from jax import lax
from jax.experimental import pallas as pl
from jax.experimental.pallas import tpu as pltpu
from jax.sharding import PartitionSpec as P

STEPS = 4
LABELS = 8
HALO = STEPS
BASE = 8
MESH = pl.DeviceIdType.MESH
GROUPS = ((0, 3), (3, 6), (6, 9))
VX, VY, VZ, SXX, SYY, SZZ, SXY, SXZ, SYZ = range(9)


def kernel(nx, ny, fields, labels, buoy_t, lame_t, shear_t, relax_t, out, state, tissue,
           buoy, lame, shear, keep, send_sem, recv_sem, local_sem):
    local_x, local_y = labels.shape[0], labels.shape[1]
    gx, gy = lax.axis_index("gx"), lax.axis_index("gy")
    has = {("gx", -1): gx > 0, ("gx", 1): gx < nx - 1, ("gy", -1): gy > 0, ("gy", 1): gy < ny - 1}
    place = {"gx": gx, "gy": gy}
    x0, x1, x2, x3 = 0, HALO, HALO + local_x, local_x + 2 * HALO
    y0, y1, y2, y3 = BASE, BASE + HALO, BASE + HALO + local_y, BASE + local_y + 2 * HALO

    own = [
        pltpu.make_async_copy(labels, tissue.at[x1:x2, y1:y2], local_sem.at[0]),
        pltpu.make_async_copy(fields, state.at[:, x1:x2, y1:y2], local_sem.at[1]),
    ]
    for copy in own:
        copy.start()

    barrier = pltpu.get_barrier_semaphore()
    for (axis, way), there in has.items():
        @pl.when(there)
        def _(axis=axis, way=way):
            pl.semaphore_signal(barrier, inc=1, device_id={axis: place[axis] + way}, device_id_type=MESH)
    pl.semaphore_wait(barrier, sum(there.astype(jnp.int32) for there in has.values()))

    count = [0]

    def remote(src, dst, axis, way):
        index = count[0]
        count[0] += 1
        return pltpu.make_async_remote_copy(
            src_ref=src, dst_ref=dst, send_sem=send_sem.at[index], recv_sem=recv_sem.at[index],
            device_id={axis: place[axis] + way}, device_id_type=MESH,
        )

    def views(source, padded):
        return {
            ("gy", 1): (source(0, local_x, local_y - HALO, local_y), padded(x1, x2, y0, y1)),
            ("gy", -1): (source(0, local_x, 0, HALO), padded(x1, x2, y2, y3)),
            ("gx", 1): (source(local_x - HALO, local_x, 0, local_y), padded(x0, x1, y1, y2)),
            ("gx", -1): (source(0, HALO, 0, local_y), padded(x2, x3, y1, y2)),
        }

    def corners(padded):
        result = {}
        for side, (low, high) in ((-1, (y0, y1)), (1, (y2, y3))):
            result[side, 1] = (padded(x2 - HALO, x2, low, high), padded(x0, x1, low, high))
            result[side, -1] = (padded(x1, x1 + HALO, low, high), padded(x2, x3, low, high))
        return result

    parts = [(lambda a, b, c, d: labels.at[a:b, c:d], lambda a, b, c, d: tissue.at[a:b, c:d])]
    for first, last in GROUPS:
        parts.append((
            lambda a, b, c, d, first=first, last=last: fields.at[first:last, a:b, c:d],
            lambda a, b, c, d, first=first, last=last: state.at[first:last, a:b, c:d],
        ))
    direct, onward = [], []
    for source, padded in parts:
        direct.append({key: remote(*pair, *key) for key, pair in views(source, padded).items()})
        onward.append({key: remote(*pair, "gx", key[1]) for key, pair in corners(padded).items()})

    for sends in direct:
        for key, copy in sends.items():
            pl.when(has[key])(copy.start)

    def blank(a, b, c, d):
        state[:, a:b, c:d] = jnp.zeros((9, b - a, d - c, state.shape[3]), jnp.float32)
        tissue[a:b, c:d] = jnp.full((b - a, d - c, tissue.shape[2]), LABELS, jnp.int32)

    pl.when(jnp.logical_not(has["gx", -1]))(lambda: blank(x0, x1, y0, y3))
    pl.when(jnp.logical_not(has["gx", 1]))(lambda: blank(x2, x3, y0, y3))
    pl.when(jnp.logical_not(has["gy", -1]))(lambda: blank(x0, x3, y0, y1))
    pl.when(jnp.logical_not(has["gy", 1]))(lambda: blank(x0, x3, y2, y3))

    for sends, passes in zip(direct, onward):
        for side in (-1, 1):
            @pl.when(has["gy", side])
            def _(sends=sends, passes=passes, side=side):
                sends["gy", -side].wait_recv()
                for way in (1, -1):
                    pl.when(has["gx", way])(passes[side, way].start)

    def arrived(index):
        for way in (1, -1):
            pl.when(has["gx", -way])(direct[index]["gx", way].wait_recv)
            for side in (-1, 1):
                pl.when(has["gx", -way] & has["gy", side])(onward[index][side, way].wait_recv)

    own[0].wait()
    arrived(0)
    rows = slice(y0, y3)

    @pl.loop(x0, x3)
    def _(p):
        label = tissue[p, rows]
        tables = [jnp.zeros(label.shape, jnp.float32) for _ in range(4)]
        for kind in range(LABELS):
            here = label == kind
            values = (buoy_t[kind], lame_t[kind], shear_t[kind], 1.0 - relax_t[kind])
            tables = [jnp.where(here, value, old) for value, old in zip(values, tables)]
        buoy[p], lame[p], shear[p], keep[p] = tables

    own[1].wait()
    for index in range(1, len(parts)):
        arrived(index)
    for passes in onward:
        for (side, way), copy in passes.items():
            pl.when(has["gy", side] & has["gx", way])(copy.wait_send)

    lanes = state.shape[3]
    lane = lax.broadcasted_iota(jnp.int32, (y3 - y0, lanes), 1)
    first_z, last_z = lane == 0, lane == lanes - 1

    def load(f, p, low, high, shift=0):
        return state[f, p, low + shift:high + shift]

    def ahead_z(a):
        following = pltpu.roll(a, lanes - 1, 1)
        return jnp.where(last_z[:a.shape[0]], 0.0, following) - a

    def behind_z(a):
        return a - jnp.where(first_z[:a.shape[0]], 0.0, pltpu.roll(a, 1, 1))

    for left in range(STEPS, 0, -1):
        low, high = x1 - left, x2 + left - 2

        @pl.loop(low, high + 1)
        def _(p):
            get = lambda f, q, shift=0: load(f, q, y0, y3, shift)
            q = p + 1
            sxy, sxz = get(SXY, p), get(SXZ, p)
            state[VX, p, rows] = get(VX, p) + buoy[p] * (
                get(SXX, q) - get(SXX, p) + (sxy - get(SXY, p, -1)) + behind_z(sxz))
            syz = get(SYZ, q)
            state[VY, q, rows] = get(VY, q) + buoy[q] * (
                get(SXY, q) - sxy + (get(SYY, q, 1) - get(SYY, q)) + behind_z(syz))
            state[VZ, q, rows] = get(VZ, q) + buoy[q] * (
                get(SXZ, q) - sxz + (syz - get(SYZ, q, -1)) + ahead_z(get(SZZ, q)))

        last = left == 1

        @pl.loop(low + 1, high + 1)
        def _(p):
            a, b = (y1, y2) if last else (y0, y3)
            get = lambda f, q, shift=0: load(f, q, a, b, shift)
            part = slice(a - y0, b - y0)
            vx, vy, vz = get(VX, p), get(VY, p), get(VZ, p)
            lam, mu, kept = lame[p, part], shear[p, part], keep[p, part]
            exx, eyy, ezz = vx - get(VX, p - 1), vy - get(VY, p, -1), behind_z(vz)
            spread = lam * (exx + eyy + ezz)
            twice = 2.0 * mu
            new = {
                SXX: kept * get(SXX, p) + spread + twice * exx,
                SYY: kept * get(SYY, p) + spread + twice * eyy,
                SZZ: kept * get(SZZ, p) + spread + twice * ezz,
                SXY: kept * get(SXY, p) + mu * (get(VX, p, 1) - vx + (get(VY, p + 1) - vy)),
                SXZ: kept * get(SXZ, p) + mu * (ahead_z(vx) + (get(VZ, p + 1) - vz)),
                SYZ: kept * get(SYZ, p) + mu * (ahead_z(vy) + (get(VZ, p, 1) - vz)),
            }
            if last:
                new.update({VX: vx, VY: vy, VZ: vz})
            for f, value in new.items():
                if last:
                    out[f, p - x1] = value
                else:
                    state[f, p, rows] = value

    for sends in direct:
        for key, copy in sends.items():
            pl.when(has[key])(copy.wait_send)


def on_device(nx, ny, fields, labels, buoyancy, lame_first, shear_modulus, relax_rate):
    local_x, local_y, lanes = labels.shape
    wide = local_x + 2 * HALO
    tall = local_y + 2 * HALO
    padded = 2 * BASE + tall
    copies = 8 * (len(GROUPS) + 1)
    anywhere = pl.BlockSpec(memory_space=pl.ANY)
    table = pl.BlockSpec(memory_space=pltpu.SMEM)
    return pl.pallas_call(
        functools.partial(kernel, nx, ny),
        out_shape=jax.ShapeDtypeStruct(fields.shape, jnp.float32),
        in_specs=[anywhere, anywhere, table, table, table, table],
        out_specs=pl.BlockSpec(memory_space=pltpu.VMEM),
        scratch_shapes=[
            pltpu.VMEM((9, wide, padded, lanes), jnp.float32),
            pltpu.VMEM((wide, padded, lanes), jnp.int32),
            pltpu.VMEM((wide, tall, lanes), jnp.float32),
            pltpu.VMEM((wide, tall, lanes), jnp.float32),
            pltpu.VMEM((wide, tall, lanes), jnp.float32),
            pltpu.VMEM((wide, tall, lanes), jnp.float32),
            pltpu.SemaphoreType.DMA((copies,)),
            pltpu.SemaphoreType.DMA((copies,)),
            pltpu.SemaphoreType.DMA((2,)),
        ],
        compiler_params=pltpu.CompilerParams(collective_id=0, has_side_effects=True),
        name="waves",
    )(fields, labels, buoyancy, lame_first, shear_modulus, relax_rate)


def solution(mesh):
    placed = (P(None, "gx", "gy", None), P("gx", "gy", None), P(), P(), P(), P())
    return jax.shard_map(
        functools.partial(on_device, mesh.shape["gx"], mesh.shape["gy"]),
        mesh=mesh, in_specs=placed, out_specs=P(None, "gx", "gy", None), check_vma=False,
    )
```

```python
import functools

import jax
import jax.numpy as jnp
from jax import lax
from jax.experimental import pallas as pl
from jax.experimental.pallas import tpu as pltpu
from jax.sharding import PartitionSpec as P

STEPS = 4
LABELS = 8
HALO = STEPS
BASE = 8
MESH = pl.DeviceIdType.MESH
GROUPS = ((0, 3), (3, 6), (6, 9))
VX, VY, VZ, SXX, SYY, SZZ, SXY, SXZ, SYZ = range(9)


def kernel(nx, ny, fields, labels, buoy_t, lame_t, shear_t, relax_t, out, state, tissue,
           buoy, lame, shear, keep, send_sem, recv_sem, local_sem):
    local_x, local_y = labels.shape[0], labels.shape[1]
    gx, gy = lax.axis_index("gx"), lax.axis_index("gy")
    has = {("gx", -1): gx > 0, ("gx", 1): gx < nx - 1, ("gy", -1): gy > 0, ("gy", 1): gy < ny - 1}
    place = {"gx": gx, "gy": gy}
    x0, x1, x2, x3 = 0, HALO, HALO + local_x, local_x + 2 * HALO
    y0, y1, y2, y3 = BASE, BASE + HALO, BASE + HALO + local_y, BASE + local_y + 2 * HALO

    own = [
        pltpu.make_async_copy(labels, tissue.at[x1:x2, y1:y2], local_sem.at[0]),
        pltpu.make_async_copy(fields, state.at[:, x1:x2, y1:y2], local_sem.at[1]),
    ]
    for copy in own:
        copy.start()

    barrier = pltpu.get_barrier_semaphore()
    for (axis, way), there in has.items():
        @pl.when(there)
        def _(axis=axis, way=way):
            pl.semaphore_signal(barrier, inc=1, device_id={axis: place[axis] + way}, device_id_type=MESH)
    pl.semaphore_wait(barrier, sum(there.astype(jnp.int32) for there in has.values()))

    count = [0]

    def remote(src, dst, axis, way):
        index = count[0]
        count[0] += 1
        return pltpu.make_async_remote_copy(
            src_ref=src, dst_ref=dst, send_sem=send_sem.at[index], recv_sem=recv_sem.at[index],
            device_id={axis: place[axis] + way}, device_id_type=MESH,
        )

    def views(source, padded):
        return {
            ("gy", 1): (source(0, local_x, local_y - HALO, local_y), padded(x1, x2, y0, y1)),
            ("gy", -1): (source(0, local_x, 0, HALO), padded(x1, x2, y2, y3)),
            ("gx", 1): (source(local_x - HALO, local_x, 0, local_y), padded(x0, x1, y1, y2)),
            ("gx", -1): (source(0, HALO, 0, local_y), padded(x2, x3, y1, y2)),
        }

    def corners(padded):
        result = {}
        for side, (low, high) in ((-1, (y0, y1)), (1, (y2, y3))):
            result[side, 1] = (padded(x2 - HALO, x2, low, high), padded(x0, x1, low, high))
            result[side, -1] = (padded(x1, x1 + HALO, low, high), padded(x2, x3, low, high))
        return result

    parts = [(lambda a, b, c, d: labels.at[a:b, c:d], lambda a, b, c, d: tissue.at[a:b, c:d])]
    for first, last in GROUPS:
        parts.append((
            lambda a, b, c, d, first=first, last=last: fields.at[first:last, a:b, c:d],
            lambda a, b, c, d, first=first, last=last: state.at[first:last, a:b, c:d],
        ))
    direct, onward = [], []
    for source, padded in parts:
        direct.append({key: remote(*pair, *key) for key, pair in views(source, padded).items()})
        onward.append({key: remote(*pair, "gx", key[1]) for key, pair in corners(padded).items()})

    for sends in direct:
        for key, copy in sends.items():
            pl.when(has[key])(copy.start)

    def blank(a, b, c, d):
        state[:, a:b, c:d] = jnp.zeros((9, b - a, d - c, state.shape[3]), jnp.float32)
        tissue[a:b, c:d] = jnp.full((b - a, d - c, tissue.shape[2]), LABELS, jnp.int32)

    pl.when(jnp.logical_not(has["gx", -1]))(lambda: blank(x0, x1, y0, y3))
    pl.when(jnp.logical_not(has["gx", 1]))(lambda: blank(x2, x3, y0, y3))
    pl.when(jnp.logical_not(has["gy", -1]))(lambda: blank(x0, x3, y0, y1))
    pl.when(jnp.logical_not(has["gy", 1]))(lambda: blank(x0, x3, y2, y3))

    def pass_on(index):
        for side in (-1, 1):
            @pl.when(has["gy", side])
            def _(side=side):
                direct[index]["gy", -side].wait_recv()
                for way in (1, -1):
                    pl.when(has["gx", way])(onward[index][side, way].start)

    def arrived(index):
        for way in (1, -1):
            pl.when(has["gx", -way])(direct[index]["gx", way].wait_recv)
            for side in (-1, 1):
                pl.when(has["gx", -way] & has["gy", side])(onward[index][side, way].wait_recv)

    pass_on(0)
    own[0].wait()
    arrived(0)
    rows = slice(y0, y3)
    pack = 2 if local_x % 2 == 0 else 1

    def each(low, count, body):
        @pl.loop(0, count // pack)
        def _(turn):
            stores = []
            for extra in range(pack):
                stores += body(low + turn * pack + extra)
            for ref, index, value in stores:
                ref[index] = value

    def look_up(p):
        label = tissue[p, rows]
        tables = [jnp.zeros(label.shape, jnp.float32) for _ in range(4)]
        for kind in range(LABELS):
            here = label == kind
            values = (buoy_t[kind], lame_t[kind], shear_t[kind], 1.0 - relax_t[kind])
            tables = [jnp.where(here, value, old) for value, old in zip(values, tables)]
        return [(ref, (p,), table) for ref, table in zip((buoy, lame, shear, keep), tables)]

    each(x0, x3 - x0, look_up)

    for index in range(1, len(parts)):
        pass_on(index)
    own[1].wait()
    for index in range(1, len(parts)):
        arrived(index)
    for passes in onward:
        for (side, way), copy in passes.items():
            pl.when(has["gy", side] & has["gx", way])(copy.wait_send)

    lanes = state.shape[3]
    lane = lax.broadcasted_iota(jnp.int32, (y3 - y0, lanes), 1)
    first_z, last_z = lane == 0, lane == lanes - 1

    def load(f, p, low, high, shift=0):
        return state[f, p, low + shift:high + shift]

    def ahead_z(a):
        following = pltpu.roll(a, lanes - 1, 1)
        return jnp.where(last_z[:a.shape[0]], 0.0, following) - a

    def behind_z(a):
        return a - jnp.where(first_z[:a.shape[0]], 0.0, pltpu.roll(a, 1, 1))

    for left in range(STEPS, 0, -1):
        low = x1 - left
        span = local_x + 2 * left

        def speeds(p):
            get = lambda f, q, shift=0: load(f, q, y0, y3, shift)
            q = p + 1
            sxy, sxz = get(SXY, p), get(SXZ, p)
            vx = get(VX, p) + buoy[p] * (
                get(SXX, q) - get(SXX, p) + (sxy - get(SXY, p, -1)) + behind_z(sxz))
            syz = get(SYZ, q)
            vy = get(VY, q) + buoy[q] * (
                get(SXY, q) - sxy + (get(SYY, q, 1) - get(SYY, q)) + behind_z(syz))
            vz = get(VZ, q) + buoy[q] * (
                get(SXZ, q) - sxz + (syz - get(SYZ, q, -1)) + ahead_z(get(SZZ, q)))
            return [(state, (VX, p, rows), vx), (state, (VY, q, rows), vy), (state, (VZ, q, rows), vz)]

        each(low, span, speeds)

        last = left == 1

        def stresses(p, last=last):
            a, b = (y1, y2) if last else (y0, y3)
            get = lambda f, q, shift=0: load(f, q, a, b, shift)
            part = slice(a - y0, b - y0)
            vx, vy, vz = get(VX, p), get(VY, p), get(VZ, p)
            lam, mu, kept = lame[p, part], shear[p, part], keep[p, part]
            exx, eyy, ezz = vx - get(VX, p - 1), vy - get(VY, p, -1), behind_z(vz)
            spread = lam * (exx + eyy + ezz)
            twice = 2.0 * mu
            new = {
                SXX: kept * get(SXX, p) + spread + twice * exx,
                SYY: kept * get(SYY, p) + spread + twice * eyy,
                SZZ: kept * get(SZZ, p) + spread + twice * ezz,
                SXY: kept * get(SXY, p) + mu * (get(VX, p, 1) - vx + (get(VY, p + 1) - vy)),
                SXZ: kept * get(SXZ, p) + mu * (ahead_z(vx) + (get(VZ, p + 1) - vz)),
                SYZ: kept * get(SYZ, p) + mu * (ahead_z(vy) + (get(VZ, p, 1) - vz)),
            }
            if last:
                new.update({VX: vx, VY: vy, VZ: vz})
            if last:
                return [(out, (f, p - x1), value) for f, value in new.items()]
            return [(state, (f, p, rows), value) for f, value in new.items()]

        each(low + 1, span - 2, stresses)

    for sends in direct:
        for key, copy in sends.items():
            pl.when(has[key])(copy.wait_send)


def on_device(nx, ny, fields, labels, buoyancy, lame_first, shear_modulus, relax_rate):
    local_x, local_y, lanes = labels.shape
    wide = local_x + 2 * HALO
    tall = local_y + 2 * HALO
    padded = 2 * BASE + tall
    copies = 8 * (len(GROUPS) + 1)
    anywhere = pl.BlockSpec(memory_space=pl.ANY)
    table = pl.BlockSpec(memory_space=pltpu.SMEM)
    return pl.pallas_call(
        functools.partial(kernel, nx, ny),
        out_shape=pltpu.VMEM(fields.shape, jnp.float32),
        in_specs=[anywhere, anywhere, table, table, table, table],
        out_specs=pl.BlockSpec(memory_space=pltpu.VMEM),
        scratch_shapes=[
            pltpu.VMEM((9, wide + 1, padded, lanes), jnp.float32),
            pltpu.VMEM((wide, padded, lanes), jnp.int32),
            pltpu.VMEM((wide + 1, tall, lanes), jnp.float32),
            pltpu.VMEM((wide + 1, tall, lanes), jnp.float32),
            pltpu.VMEM((wide + 1, tall, lanes), jnp.float32),
            pltpu.VMEM((wide + 1, tall, lanes), jnp.float32),
            pltpu.SemaphoreType.DMA((copies,)),
            pltpu.SemaphoreType.DMA((copies,)),
            pltpu.SemaphoreType.DMA((2,)),
        ],
        compiler_params=pltpu.CompilerParams(collective_id=0, has_side_effects=True),
        name="waves",
    )(fields, labels, buoyancy, lame_first, shear_modulus, relax_rate)


def solution(mesh):
    placed = (P(None, "gx", "gy", None), P("gx", "gy", None), P(), P(), P(), P())
    return jax.shard_map(
        functools.partial(on_device, mesh.shape["gx"], mesh.shape["gy"]),
        mesh=mesh, in_specs=placed, out_specs=P(None, "gx", "gy", None), check_vma=False,
    )
```

```python
import functools

import jax
import jax.numpy as jnp
from jax import lax
from jax.experimental import pallas as pl
from jax.experimental.pallas import tpu as pltpu
from jax.sharding import PartitionSpec as P

STEPS = 4
LABELS = 8
HALO = STEPS
BASE = 8
MESH = pl.DeviceIdType.MESH
GROUPS = ((0, 3), (3, 6), (6, 9))
VX, VY, VZ, SXX, SYY, SZZ, SXY, SXZ, SYZ = range(9)


def kernel(nx, ny, fields, labels, buoy_t, lame_t, shear_t, relax_t, out, state, tissue,
           buoy, lame, shear, keep, send_sem, recv_sem, local_sem):
    local_x, local_y = labels.shape[0], labels.shape[1]
    gx, gy = lax.axis_index("gx"), lax.axis_index("gy")
    has = {("gx", -1): gx > 0, ("gx", 1): gx < nx - 1, ("gy", -1): gy > 0, ("gy", 1): gy < ny - 1}
    place = {"gx": gx, "gy": gy}
    x0, x1, x2, x3 = 0, HALO, HALO + local_x, local_x + 2 * HALO
    y0, y1, y2, y3 = BASE, BASE + HALO, BASE + HALO + local_y, BASE + local_y + 2 * HALO

    own = [
        pltpu.make_async_copy(labels, tissue.at[x1:x2, y1:y2], local_sem.at[0]),
        pltpu.make_async_copy(fields, state.at[:, x1:x2, y1:y2], local_sem.at[1]),
    ]
    for copy in own:
        copy.start()

    barrier = pltpu.get_barrier_semaphore()
    for (axis, way), there in has.items():
        @pl.when(there)
        def _(axis=axis, way=way):
            pl.semaphore_signal(barrier, inc=1, device_id={axis: place[axis] + way}, device_id_type=MESH)
    pl.semaphore_wait(barrier, sum(there.astype(jnp.int32) for there in has.values()))

    count = [0]

    def remote(src, dst, axis, way):
        index = count[0]
        count[0] += 1
        return pltpu.make_async_remote_copy(
            src_ref=src, dst_ref=dst, send_sem=send_sem.at[index], recv_sem=recv_sem.at[index],
            device_id={axis: place[axis] + way}, device_id_type=MESH,
        )

    def views(source, padded):
        return {
            ("gy", 1): (source(0, local_x, local_y - HALO, local_y), padded(x1, x2, y0, y1)),
            ("gy", -1): (source(0, local_x, 0, HALO), padded(x1, x2, y2, y3)),
            ("gx", 1): (source(local_x - HALO, local_x, 0, local_y), padded(x0, x1, y1, y2)),
            ("gx", -1): (source(0, HALO, 0, local_y), padded(x2, x3, y1, y2)),
        }

    def corners(padded):
        result = {}
        for side, (low, high) in ((-1, (y0, y1)), (1, (y2, y3))):
            result[side, 1] = (padded(x2 - HALO, x2, low, high), padded(x0, x1, low, high))
            result[side, -1] = (padded(x1, x1 + HALO, low, high), padded(x2, x3, low, high))
        return result

    parts = [(lambda a, b, c, d: labels.at[a:b, c:d], lambda a, b, c, d: tissue.at[a:b, c:d])]
    for first, last in GROUPS:
        parts.append((
            lambda a, b, c, d, first=first, last=last: fields.at[first:last, a:b, c:d],
            lambda a, b, c, d, first=first, last=last: state.at[first:last, a:b, c:d],
        ))
    direct, onward = [], []
    for source, padded in parts:
        direct.append({key: remote(*pair, *key) for key, pair in views(source, padded).items()})
        onward.append({key: remote(*pair, "gx", key[1]) for key, pair in corners(padded).items()})

    for sends in direct:
        for key, copy in sends.items():
            pl.when(has[key])(copy.start)

    def blank(a, b, c, d):
        state[:, a:b, c:d] = jnp.zeros((9, b - a, d - c, state.shape[3]), jnp.float32)
        tissue[a:b, c:d] = jnp.full((b - a, d - c, tissue.shape[2]), LABELS, jnp.int32)

    pl.when(jnp.logical_not(has["gx", -1]))(lambda: blank(x0, x1, y0, y3))
    pl.when(jnp.logical_not(has["gx", 1]))(lambda: blank(x2, x3, y0, y3))
    pl.when(jnp.logical_not(has["gy", -1]))(lambda: blank(x0, x3, y0, y1))
    pl.when(jnp.logical_not(has["gy", 1]))(lambda: blank(x0, x3, y2, y3))

    def pass_on(index):
        for side in (-1, 1):
            @pl.when(has["gy", side])
            def _(side=side):
                direct[index]["gy", -side].wait_recv()
                for way in (1, -1):
                    pl.when(has["gx", way])(onward[index][side, way].start)

    def arrived(index):
        for way in (1, -1):
            pl.when(has["gx", -way])(direct[index]["gx", way].wait_recv)
            for side in (-1, 1):
                pl.when(has["gx", -way] & has["gy", side])(onward[index][side, way].wait_recv)

    pass_on(0)
    own[0].wait()
    arrived(0)
    rows = slice(y0, y3)
    pack = 2 if local_x % 2 == 0 else 1

    def each(low, count, body):
        @pl.loop(0, count // pack)
        def _(turn):
            stores = []
            for extra in range(pack):
                stores += body(low + turn * pack + extra)
            for ref, index, value in stores:
                ref[index] = value

    def look_up(p):
        label = tissue[p, rows]
        tables = [jnp.zeros(label.shape, jnp.float32) for _ in range(4)]
        for kind in range(LABELS):
            here = label == kind
            values = (buoy_t[kind], lame_t[kind], shear_t[kind], 1.0 - relax_t[kind])
            tables = [jnp.where(here, value, old) for value, old in zip(values, tables)]
        return [(ref, (p,), table) for ref, table in zip((buoy, lame, shear, keep), tables)]

    each(x0, x3 - x0, look_up)

    for index in range(1, len(parts)):
        pass_on(index)
    own[1].wait()

    def sent(index):
        for (side, way), copy in onward[index].items():
            pl.when(has["gy", side] & has["gx", way])(copy.wait_send)

    lanes = state.shape[3]
    lane = lax.broadcasted_iota(jnp.int32, (y3 - y0, lanes), 1)
    first_z, last_z = lane == 0, lane == lanes - 1

    def load(f, p, low, high, shift=0):
        return state[f, p, low + shift:high + shift]

    def ahead_z(a):
        following = pltpu.roll(a, lanes - 1, 1)
        return jnp.where(last_z[:a.shape[0]], 0.0, following) - a

    def behind_z(a):
        return a - jnp.where(first_z[:a.shape[0]], 0.0, pltpu.roll(a, 1, 1))

    def speeds(p):
        get = lambda f, q, shift=0: load(f, q, y0, y3, shift)
        q = p + 1
        sxy, sxz = get(SXY, p), get(SXZ, p)
        vx = get(VX, p) + buoy[p] * (
            get(SXX, q) - get(SXX, p) + (sxy - get(SXY, p, -1)) + behind_z(sxz))
        syz = get(SYZ, q)
        vy = get(VY, q) + buoy[q] * (
            get(SXY, q) - sxy + (get(SYY, q, 1) - get(SYY, q)) + behind_z(syz))
        vz = get(VZ, q) + buoy[q] * (
            get(SXZ, q) - sxz + (syz - get(SYZ, q, -1)) + ahead_z(get(SZZ, q)))
        return [(state, (VX, p, rows), vx), (state, (VY, q, rows), vy), (state, (VZ, q, rows), vz)]

    def stresses(last, p):
        a, b = (y1, y2) if last else (y0, y3)
        get = lambda f, q, shift=0: load(f, q, a, b, shift)
        part = slice(a - y0, b - y0)
        vx, vy, vz = get(VX, p), get(VY, p), get(VZ, p)
        lam, mu, kept = lame[p, part], shear[p, part], keep[p, part]
        exx, eyy, ezz = vx - get(VX, p - 1), vy - get(VY, p, -1), behind_z(vz)
        spread = lam * (exx + eyy + ezz)
        twice = 2.0 * mu
        new = {
            SXX: kept * get(SXX, p) + spread + twice * exx,
            SYY: kept * get(SYY, p) + spread + twice * eyy,
            SZZ: kept * get(SZZ, p) + spread + twice * ezz,
            SXY: kept * get(SXY, p) + mu * (get(VX, p, 1) - vx + (get(VY, p + 1) - vy)),
            SXZ: kept * get(SXZ, p) + mu * (ahead_z(vx) + (get(VZ, p + 1) - vz)),
            SYZ: kept * get(SYZ, p) + mu * (ahead_z(vy) + (get(VZ, p, 1) - vz)),
        }
        if last:
            new.update({VX: vx, VY: vy, VZ: vz})
        if last:
            return [(out, (f, p - x1), value) for f, value in new.items()]
        return [(state, (f, p, rows), value) for f, value in new.items()]

    def together(body, places):
        for ref, index, value in [store for p in places for store in body(p)]:
            ref[index] = value

    def sides(body, first, second):
        @pl.loop(0, HALO // 2)
        def _(turn):
            together(body, [base + 2 * turn + extra for base in (first, second) for extra in (0, 1)])

    def middle(body, first, after):
        for p in range(first, after, 2):
            together(body, range(p, min(p + 2, after)))

    sent(0)
    sent(1)
    for done in range(STEPS):
        middle(speeds, x1 + done, x2 - 1 - done)
        if done == 0:
            for index in range(2, len(parts)):
                sent(index)
        middle(functools.partial(stresses, False), x1 + 1 + done, x2 - 1 - done)

    for index in range(1, len(parts)):
        arrived(index)
    for done in range(STEPS):
        sides(speeds, x1 - HALO + done, x2 - 1 - done)
        sides(functools.partial(stresses, done == STEPS - 1), x1 - HALO + 1 + done, x2 - 1 - done)

    for sends in direct:
        for key, copy in sends.items():
            pl.when(has[key])(copy.wait_send)


def on_device(nx, ny, fields, labels, buoyancy, lame_first, shear_modulus, relax_rate):
    local_x, local_y, lanes = labels.shape
    wide = local_x + 2 * HALO
    tall = local_y + 2 * HALO
    padded = 2 * BASE + tall
    copies = 8 * (len(GROUPS) + 1)
    anywhere = pl.BlockSpec(memory_space=pl.ANY)
    table = pl.BlockSpec(memory_space=pltpu.SMEM)
    return pl.pallas_call(
        functools.partial(kernel, nx, ny),
        out_shape=pltpu.VMEM(fields.shape, jnp.float32),
        in_specs=[anywhere, anywhere, table, table, table, table],
        out_specs=pl.BlockSpec(memory_space=pltpu.VMEM),
        scratch_shapes=[
            pltpu.VMEM((9, wide + 1, padded, lanes), jnp.float32),
            pltpu.VMEM((wide, padded, lanes), jnp.int32),
            pltpu.VMEM((wide + 1, tall, lanes), jnp.float32),
            pltpu.VMEM((wide + 1, tall, lanes), jnp.float32),
            pltpu.VMEM((wide + 1, tall, lanes), jnp.float32),
            pltpu.VMEM((wide + 1, tall, lanes), jnp.float32),
            pltpu.SemaphoreType.DMA((copies,)),
            pltpu.SemaphoreType.DMA((copies,)),
            pltpu.SemaphoreType.DMA((2,)),
        ],
        compiler_params=pltpu.CompilerParams(collective_id=0, has_side_effects=True),
        name="waves",
    )(fields, labels, buoyancy, lame_first, shear_modulus, relax_rate)


def solution(mesh):
    placed = (P(None, "gx", "gy", None), P("gx", "gy", None), P(), P(), P(), P())
    return jax.shard_map(
        functools.partial(on_device, mesh.shape["gx"], mesh.shape["gy"]),
        mesh=mesh, in_specs=placed, out_specs=P(None, "gx", "gy", None), check_vma=False,
    )
```

```python
import functools

import jax
import jax.numpy as jnp
from jax import lax
from jax.experimental import pallas as pl
from jax.experimental.pallas import tpu as pltpu
from jax.sharding import PartitionSpec as P

STEPS = 4
LABELS = 8
HALO = STEPS
BASE = 8
MESH = pl.DeviceIdType.MESH
GROUPS = ((0, 3), (3, 6), (6, 9))
VX, VY, VZ, SXX, SYY, SZZ, SXY, SXZ, SYZ = range(9)


def kernel(nx, ny, fields, labels, buoy_t, lame_t, shear_t, relax_t, out, state, tissue,
           buoy, lame, shear, keep, send_sem, recv_sem, local_sem):
    local_x, local_y = labels.shape[0], labels.shape[1]
    gx, gy = lax.axis_index("gx"), lax.axis_index("gy")
    has = {("gx", -1): gx > 0, ("gx", 1): gx < nx - 1, ("gy", -1): gy > 0, ("gy", 1): gy < ny - 1}
    place = {"gx": gx, "gy": gy}
    x0, x1, x2, x3 = 0, HALO, HALO + local_x, local_x + 2 * HALO
    y0, y1, y2, y3 = BASE, BASE + HALO, BASE + HALO + local_y, BASE + local_y + 2 * HALO

    own = [
        pltpu.make_async_copy(labels, tissue.at[x1:x2, y1:y2], local_sem.at[0]),
        pltpu.make_async_copy(fields, state.at[:, x1:x2, y1:y2], local_sem.at[1]),
    ]
    for copy in own:
        copy.start()

    barrier = pltpu.get_barrier_semaphore()
    for (axis, way), there in has.items():
        @pl.when(there)
        def _(axis=axis, way=way):
            pl.semaphore_signal(barrier, inc=1, device_id={axis: place[axis] + way}, device_id_type=MESH)
    pl.semaphore_wait(barrier, sum(there.astype(jnp.int32) for there in has.values()))

    count = [0]

    def remote(src, dst, axis, way):
        index = count[0]
        count[0] += 1
        return pltpu.make_async_remote_copy(
            src_ref=src, dst_ref=dst, send_sem=send_sem.at[index], recv_sem=recv_sem.at[index],
            device_id={axis: place[axis] + way}, device_id_type=MESH,
        )

    def views(source, padded):
        return {
            ("gy", 1): (source(0, local_x, local_y - HALO, local_y), padded(x1, x2, y0, y1)),
            ("gy", -1): (source(0, local_x, 0, HALO), padded(x1, x2, y2, y3)),
            ("gx", 1): (source(local_x - HALO, local_x, 0, local_y), padded(x0, x1, y1, y2)),
            ("gx", -1): (source(0, HALO, 0, local_y), padded(x2, x3, y1, y2)),
        }

    def corners(padded):
        result = {}
        for side, (low, high) in ((-1, (y0, y1)), (1, (y2, y3))):
            result[side, 1] = (padded(x2 - HALO, x2, low, high), padded(x0, x1, low, high))
            result[side, -1] = (padded(x1, x1 + HALO, low, high), padded(x2, x3, low, high))
        return result

    parts = [(lambda a, b, c, d: labels.at[a:b, c:d], lambda a, b, c, d: tissue.at[a:b, c:d])]
    for first, last in GROUPS:
        parts.append((
            lambda a, b, c, d, first=first, last=last: fields.at[first:last, a:b, c:d],
            lambda a, b, c, d, first=first, last=last: state.at[first:last, a:b, c:d],
        ))
    direct, onward = [], []
    for source, padded in parts:
        direct.append({key: remote(*pair, *key) for key, pair in views(source, padded).items()})
        onward.append({key: remote(*pair, "gx", key[1]) for key, pair in corners(padded).items()})

    for sends in direct:
        for key, copy in sends.items():
            pl.when(has[key])(copy.start)

    def blank(a, b, c, d):
        state[:, a:b, c:d] = jnp.zeros((9, b - a, d - c, state.shape[3]), jnp.float32)
        tissue[a:b, c:d] = jnp.full((b - a, d - c, tissue.shape[2]), LABELS, jnp.int32)

    pl.when(jnp.logical_not(has["gx", -1]))(lambda: blank(x0, x1, y0, y3))
    pl.when(jnp.logical_not(has["gx", 1]))(lambda: blank(x2, x3, y0, y3))
    pl.when(jnp.logical_not(has["gy", -1]))(lambda: blank(x0, x3, y0, y1))
    pl.when(jnp.logical_not(has["gy", 1]))(lambda: blank(x0, x3, y2, y3))

    def pass_on(index):
        for side in (-1, 1):
            @pl.when(has["gy", side])
            def _(side=side):
                direct[index]["gy", -side].wait_recv()
                for way in (1, -1):
                    pl.when(has["gx", way])(onward[index][side, way].start)

    def arrived(index):
        for way in (1, -1):
            pl.when(has["gx", -way])(direct[index]["gx", way].wait_recv)
            for side in (-1, 1):
                pl.when(has["gx", -way] & has["gy", side])(onward[index][side, way].wait_recv)

    pass_on(0)
    own[0].wait()
    arrived(0)
    rows = slice(y0, y3)
    pack = 4 if local_x % 4 == 0 else 1

    def each(low, count, body):
        @pl.loop(0, count // pack)
        def _(turn):
            stores = []
            for extra in range(pack):
                stores += body(low + turn * pack + extra)
            for ref, index, value in stores:
                ref[index] = value

    def look_up(p):
        label = tissue[p, rows]
        tables = [jnp.zeros(label.shape, jnp.float32) for _ in range(4)]
        for kind in range(LABELS):
            here = label == kind
            values = (buoy_t[kind], lame_t[kind], shear_t[kind], 1.0 - relax_t[kind])
            tables = [jnp.where(here, value, old) for value, old in zip(values, tables)]
        return [(ref, (p,), table) for ref, table in zip((buoy, lame, shear, keep), tables)]

    each(x0, x3 - x0, look_up)

    for index in range(1, len(parts)):
        pass_on(index)
    own[1].wait()

    def sent(index):
        for (side, way), copy in onward[index].items():
            pl.when(has["gy", side] & has["gx", way])(copy.wait_send)

    lanes = state.shape[3]
    lane = lax.broadcasted_iota(jnp.int32, (y3 - y0, lanes), 1)
    first_z, last_z = lane == 0, lane == lanes - 1

    def load(f, p, low, high, shift=0):
        return state[f, p, low + shift:high + shift]

    def ahead_z(a):
        following = pltpu.roll(a, lanes - 1, 1)
        return jnp.where(last_z[:a.shape[0]], 0.0, following) - a

    def behind_z(a):
        return a - jnp.where(first_z[:a.shape[0]], 0.0, pltpu.roll(a, 1, 1))

    def speeds(p):
        get = lambda f, q, shift=0: load(f, q, y0, y3, shift)
        q = p + 1
        sxy, sxz = get(SXY, p), get(SXZ, p)
        vx = get(VX, p) + buoy[p] * (
            get(SXX, q) - get(SXX, p) + (sxy - get(SXY, p, -1)) + behind_z(sxz))
        syz = get(SYZ, q)
        vy = get(VY, q) + buoy[q] * (
            get(SXY, q) - sxy + (get(SYY, q, 1) - get(SYY, q)) + behind_z(syz))
        vz = get(VZ, q) + buoy[q] * (
            get(SXZ, q) - sxz + (syz - get(SYZ, q, -1)) + ahead_z(get(SZZ, q)))
        return [(state, (VX, p, rows), vx), (state, (VY, q, rows), vy), (state, (VZ, q, rows), vz)]

    def stresses(last, p):
        a, b = (y1, y2) if last else (y0, y3)
        get = lambda f, q, shift=0: load(f, q, a, b, shift)
        part = slice(a - y0, b - y0)
        vx, vy, vz = get(VX, p), get(VY, p), get(VZ, p)
        lam, mu, kept = lame[p, part], shear[p, part], keep[p, part]
        exx, eyy, ezz = vx - get(VX, p - 1), vy - get(VY, p, -1), behind_z(vz)
        spread = lam * (exx + eyy + ezz)
        twice = 2.0 * mu
        new = {
            SXX: kept * get(SXX, p) + spread + twice * exx,
            SYY: kept * get(SYY, p) + spread + twice * eyy,
            SZZ: kept * get(SZZ, p) + spread + twice * ezz,
            SXY: kept * get(SXY, p) + mu * (get(VX, p, 1) - vx + (get(VY, p + 1) - vy)),
            SXZ: kept * get(SXZ, p) + mu * (ahead_z(vx) + (get(VZ, p + 1) - vz)),
            SYZ: kept * get(SYZ, p) + mu * (ahead_z(vy) + (get(VZ, p, 1) - vz)),
        }
        if last:
            new.update({VX: vx, VY: vy, VZ: vz})
        if last:
            return [(out, (f, p - x1), value) for f, value in new.items()]
        return [(state, (f, p, rows), value) for f, value in new.items()]

    def together(body, places):
        for ref, index, value in [store for p in places for store in body(p)]:
            ref[index] = value

    def sides(body, first, second):
        together(body, [base + extra for base in (first, second) for extra in range(HALO)])

    def middle(body, first, after):
        for p in range(first, after, 2):
            together(body, range(p, min(p + 2, after)))

    sent(0)
    sent(1)
    for done in range(STEPS):
        middle(speeds, x1 + done, x2 - 1 - done)
        if done == 0:
            for index in range(2, len(parts)):
                sent(index)
        middle(functools.partial(stresses, False), x1 + 1 + done, x2 - 1 - done)

    for index in range(1, len(parts)):
        arrived(index)
    for done in range(STEPS):
        sides(speeds, x1 - HALO + done, x2 - 1 - done)
        sides(functools.partial(stresses, done == STEPS - 1), x1 - HALO + 1 + done, x2 - 1 - done)

    for sends in direct:
        for key, copy in sends.items():
            pl.when(has[key])(copy.wait_send)


def on_device(nx, ny, fields, labels, buoyancy, lame_first, shear_modulus, relax_rate):
    local_x, local_y, lanes = labels.shape
    wide = local_x + 2 * HALO
    tall = local_y + 2 * HALO
    padded = 2 * BASE + tall
    copies = 8 * (len(GROUPS) + 1)
    anywhere = pl.BlockSpec(memory_space=pl.ANY)
    table = pl.BlockSpec(memory_space=pltpu.SMEM)
    return pl.pallas_call(
        functools.partial(kernel, nx, ny),
        out_shape=pltpu.VMEM(fields.shape, jnp.float32),
        in_specs=[anywhere, anywhere, table, table, table, table],
        out_specs=pl.BlockSpec(memory_space=pltpu.VMEM),
        scratch_shapes=[
            pltpu.VMEM((9, wide + 1, padded, lanes), jnp.float32),
            pltpu.VMEM((wide, padded, lanes), jnp.int32),
            pltpu.VMEM((wide + 1, tall, lanes), jnp.float32),
            pltpu.VMEM((wide + 1, tall, lanes), jnp.float32),
            pltpu.VMEM((wide + 1, tall, lanes), jnp.float32),
            pltpu.VMEM((wide + 1, tall, lanes), jnp.float32),
            pltpu.SemaphoreType.DMA((copies,)),
            pltpu.SemaphoreType.DMA((copies,)),
            pltpu.SemaphoreType.DMA((2,)),
        ],
        compiler_params=pltpu.CompilerParams(collective_id=0, has_side_effects=True),
        name="waves",
    )(fields, labels, buoyancy, lame_first, shear_modulus, relax_rate)


def solution(mesh):
    placed = (P(None, "gx", "gy", None), P("gx", "gy", None), P(), P(), P(), P())
    return jax.shard_map(
        functools.partial(on_device, mesh.shape["gx"], mesh.shape["gy"]),
        mesh=mesh, in_specs=placed, out_specs=P(None, "gx", "gy", None), check_vma=False,
    )
```

```python
import functools

import jax
import jax.numpy as jnp
from jax import lax
from jax.experimental import pallas as pl
from jax.experimental.pallas import tpu as pltpu
from jax.sharding import PartitionSpec as P

STEPS = 4
LABELS = 8
HALO = STEPS
BASE = 8
MESH = pl.DeviceIdType.MESH
GROUPS = ((0, 4), (4, 7), (7, 9))
VX, VY, VZ, SXX, SYY, SZZ, SXY, SXZ, SYZ = range(9)


def kernel(nx, ny, fields, labels, buoy_t, lame_t, shear_t, relax_t, out, state, tissue,
           buoy, lame, shear, keep, send_sem, recv_sem, local_sem):
    local_x, local_y = labels.shape[0], labels.shape[1]
    gx, gy = lax.axis_index("gx"), lax.axis_index("gy")
    has = {("gx", -1): gx > 0, ("gx", 1): gx < nx - 1, ("gy", -1): gy > 0, ("gy", 1): gy < ny - 1}
    place = {"gx": gx, "gy": gy}
    x0, x1, x2, x3 = 0, HALO, HALO + local_x, local_x + 2 * HALO
    y0, y1, y2, y3 = BASE, BASE + HALO, BASE + HALO + local_y, BASE + local_y + 2 * HALO

    own = [
        pltpu.make_async_copy(labels, tissue.at[x1:x2, y1:y2], local_sem.at[0]),
        pltpu.make_async_copy(fields, state.at[:, x1:x2, y1:y2], local_sem.at[1]),
    ]
    for copy in own:
        copy.start()

    barrier = pltpu.get_barrier_semaphore()
    for (axis, way), there in has.items():
        @pl.when(there)
        def _(axis=axis, way=way):
            pl.semaphore_signal(barrier, inc=1, device_id={axis: place[axis] + way}, device_id_type=MESH)
    pl.semaphore_wait(barrier, sum(there.astype(jnp.int32) for there in has.values()))

    count = [0]

    def remote(src, dst, axis, way):
        index = count[0]
        count[0] += 1
        return pltpu.make_async_remote_copy(
            src_ref=src, dst_ref=dst, send_sem=send_sem.at[index], recv_sem=recv_sem.at[index],
            device_id={axis: place[axis] + way}, device_id_type=MESH,
        )

    def views(source, padded):
        return {
            ("gy", 1): (source(0, local_x, local_y - HALO, local_y), padded(x1, x2, y0, y1)),
            ("gy", -1): (source(0, local_x, 0, HALO), padded(x1, x2, y2, y3)),
            ("gx", 1): (source(local_x - HALO, local_x, 0, local_y), padded(x0, x1, y1, y2)),
            ("gx", -1): (source(0, HALO, 0, local_y), padded(x2, x3, y1, y2)),
        }

    def corners(padded):
        result = {}
        for side, (low, high) in ((-1, (y0, y1)), (1, (y2, y3))):
            result[side, 1] = (padded(x2 - HALO, x2, low, high), padded(x0, x1, low, high))
            result[side, -1] = (padded(x1, x1 + HALO, low, high), padded(x2, x3, low, high))
        return result

    parts = [(lambda a, b, c, d: labels.at[a:b, c:d], lambda a, b, c, d: tissue.at[a:b, c:d])]
    for first, last in GROUPS:
        parts.append((
            lambda a, b, c, d, first=first, last=last: fields.at[first:last, a:b, c:d],
            lambda a, b, c, d, first=first, last=last: state.at[first:last, a:b, c:d],
        ))
    direct, onward = [], []
    for source, padded in parts:
        direct.append({key: remote(*pair, *key) for key, pair in views(source, padded).items()})
        onward.append({key: remote(*pair, "gx", key[1]) for key, pair in corners(padded).items()})

    for key, copy in direct[0].items():
        pl.when(has[key])(copy.start)
    for axis in ("gy", "gx"):
        for sends in direct[1:]:
            for way in (1, -1):
                pl.when(has[axis, way])(sends[axis, way].start)

    def blank(a, b, c, d):
        state[:, a:b, c:d] = jnp.zeros((9, b - a, d - c, state.shape[3]), jnp.float32)
        tissue[a:b, c:d] = jnp.full((b - a, d - c, tissue.shape[2]), LABELS, jnp.int32)

    pl.when(jnp.logical_not(has["gx", -1]))(lambda: blank(x0, x1, y0, y3))
    pl.when(jnp.logical_not(has["gx", 1]))(lambda: blank(x2, x3, y0, y3))
    pl.when(jnp.logical_not(has["gy", -1]))(lambda: blank(x0, x3, y0, y1))
    pl.when(jnp.logical_not(has["gy", 1]))(lambda: blank(x0, x3, y2, y3))

    def pass_on(index):
        for side in (-1, 1):
            @pl.when(has["gy", side])
            def _(side=side):
                direct[index]["gy", -side].wait_recv()
                for way in (1, -1):
                    pl.when(has["gx", way])(onward[index][side, way].start)

    def arrived(index):
        for way in (1, -1):
            pl.when(has["gx", -way])(direct[index]["gx", way].wait_recv)
            for side in (-1, 1):
                pl.when(has["gx", -way] & has["gy", side])(onward[index][side, way].wait_recv)

    pass_on(0)
    own[0].wait()
    arrived(0)
    rows = slice(y0, y3)
    pack = 4 if local_x % 4 == 0 else 1

    def each(low, count, body):
        @pl.loop(0, count // pack)
        def _(turn):
            stores = []
            for extra in range(pack):
                stores += body(low + turn * pack + extra)
            for ref, index, value in stores:
                ref[index] = value

    def look_up(p):
        label = tissue[p, rows]
        tables = [jnp.zeros(label.shape, jnp.float32) for _ in range(4)]
        for kind in range(LABELS):
            here = label == kind
            values = (buoy_t[kind], lame_t[kind], shear_t[kind], 1.0 - relax_t[kind])
            tables = [jnp.where(here, value, old) for value, old in zip(values, tables)]
        return [(ref, (p,), table) for ref, table in zip((buoy, lame, shear, keep), tables)]

    each(x0, x3 - x0, look_up)

    for index in range(1, len(parts)):
        pass_on(index)
    own[1].wait()

    def sent(index):
        for (side, way), copy in onward[index].items():
            pl.when(has["gy", side] & has["gx", way])(copy.wait_send)

    lanes = state.shape[3]
    lane = lax.broadcasted_iota(jnp.int32, (y3 - y0, lanes), 1)
    first_z, last_z = lane == 0, lane == lanes - 1

    def load(f, p, low, high, shift=0):
        return state[f, p, low + shift:high + shift]

    def ahead_z(a):
        following = pltpu.roll(a, lanes - 1, 1)
        return jnp.where(last_z[:a.shape[0]], 0.0, following) - a

    def behind_z(a):
        return a - jnp.where(first_z[:a.shape[0]], 0.0, pltpu.roll(a, 1, 1))

    def speeds(p):
        get = lambda f, q, shift=0: load(f, q, y0, y3, shift)
        q = p + 1
        sxy, sxz = get(SXY, p), get(SXZ, p)
        vx = get(VX, p) + buoy[p] * (
            get(SXX, q) - get(SXX, p) + (sxy - get(SXY, p, -1)) + behind_z(sxz))
        syz = get(SYZ, q)
        vy = get(VY, q) + buoy[q] * (
            get(SXY, q) - sxy + (get(SYY, q, 1) - get(SYY, q)) + behind_z(syz))
        vz = get(VZ, q) + buoy[q] * (
            get(SXZ, q) - sxz + (syz - get(SYZ, q, -1)) + ahead_z(get(SZZ, q)))
        return [(state, (VX, p, rows), vx), (state, (VY, q, rows), vy), (state, (VZ, q, rows), vz)]

    def stresses(last, p):
        a, b = (y1, y2) if last else (y0, y3)
        get = lambda f, q, shift=0: load(f, q, a, b, shift)
        part = slice(a - y0, b - y0)
        vx, vy, vz = get(VX, p), get(VY, p), get(VZ, p)
        lam, mu, kept = lame[p, part], shear[p, part], keep[p, part]
        exx, eyy, ezz = vx - get(VX, p - 1), vy - get(VY, p, -1), behind_z(vz)
        spread = lam * (exx + eyy + ezz)
        twice = 2.0 * mu
        new = {
            SXX: kept * get(SXX, p) + spread + twice * exx,
            SYY: kept * get(SYY, p) + spread + twice * eyy,
            SZZ: kept * get(SZZ, p) + spread + twice * ezz,
            SXY: kept * get(SXY, p) + mu * (get(VX, p, 1) - vx + (get(VY, p + 1) - vy)),
            SXZ: kept * get(SXZ, p) + mu * (ahead_z(vx) + (get(VZ, p + 1) - vz)),
            SYZ: kept * get(SYZ, p) + mu * (ahead_z(vy) + (get(VZ, p, 1) - vz)),
        }
        if last:
            new.update({VX: vx, VY: vy, VZ: vz})
        if last:
            return [(out, (f, p - x1), value) for f, value in new.items()]
        return [(state, (f, p, rows), value) for f, value in new.items()]

    def together(body, places):
        for ref, index, value in [store for p in places for store in body(p)]:
            ref[index] = value

    def sides(body, first, second):
        together(body, [base + extra for base in (first, second) for extra in range(HALO)])

    def middle(body, first, after):
        for p in range(first, after, 2):
            together(body, range(p, min(p + 2, after)))

    sent(0)
    sent(1)
    for done in range(STEPS):
        middle(speeds, x1 + done, x2 - 1 - done)
        if done == 0:
            for index in range(2, len(parts)):
                sent(index)
        middle(functools.partial(stresses, False), x1 + 1 + done, x2 - 1 - done)

    for index in range(1, len(parts)):
        arrived(index)
    for done in range(STEPS):
        sides(speeds, x1 - HALO + done, x2 - 1 - done)
        sides(functools.partial(stresses, done == STEPS - 1), x1 - HALO + 1 + done, x2 - 1 - done)

    for sends in direct:
        for key, copy in sends.items():
            pl.when(has[key])(copy.wait_send)


def on_device(nx, ny, fields, labels, buoyancy, lame_first, shear_modulus, relax_rate):
    local_x, local_y, lanes = labels.shape
    wide = local_x + 2 * HALO
    tall = local_y + 2 * HALO
    padded = 2 * BASE + tall
    copies = 8 * (len(GROUPS) + 1)
    anywhere = pl.BlockSpec(memory_space=pl.ANY)
    table = pl.BlockSpec(memory_space=pltpu.SMEM)
    return pl.pallas_call(
        functools.partial(kernel, nx, ny),
        out_shape=pltpu.VMEM(fields.shape, jnp.float32),
        in_specs=[anywhere, anywhere, table, table, table, table],
        out_specs=pl.BlockSpec(memory_space=pltpu.VMEM),
        scratch_shapes=[
            pltpu.VMEM((9, wide + 1, padded, lanes), jnp.float32),
            pltpu.VMEM((wide, padded, lanes), jnp.int32),
            pltpu.VMEM((wide + 1, tall, lanes), jnp.float32),
            pltpu.VMEM((wide + 1, tall, lanes), jnp.float32),
            pltpu.VMEM((wide + 1, tall, lanes), jnp.float32),
            pltpu.VMEM((wide + 1, tall, lanes), jnp.float32),
            pltpu.SemaphoreType.DMA((copies,)),
            pltpu.SemaphoreType.DMA((copies,)),
            pltpu.SemaphoreType.DMA((2,)),
        ],
        compiler_params=pltpu.CompilerParams(collective_id=0, has_side_effects=True),
        name="waves",
    )(fields, labels, buoyancy, lame_first, shear_modulus, relax_rate)


def solution(mesh):
    placed = (P(None, "gx", "gy", None), P("gx", "gy", None), P(), P(), P(), P())
    return jax.shard_map(
        functools.partial(on_device, mesh.shape["gx"], mesh.shape["gy"]),
        mesh=mesh, in_specs=placed, out_specs=P(None, "gx", "gy", None), check_vma=False,
    )
```
